256 devices in a mesh: blk: 64 (over z, x, y_lo), lane: 4 (over y_hi, core).
Axes of the slice: x: 4, y: 4 (y_hi: 2, y_lo: 2; y = y_hi * 2 + y_lo), z: 8, core: 2. Of those that a mesh axis runs over, the one named last changes fastest.
Arguments:
- features: float32 [98304, 512], P(('blk', 'lane')), may hold values from -6 to 6
- weight: float32 [512, 512], replicated, may hold values from -0.25 to 0.25
- hub_values: float32 [3, 98304, 1536], P(None, 'blk', 'lane'), may hold values from -0.125 to 0.125
- hub_mask: int32 [3, 768, 12], P(None, 'blk', 'lane'), may hold values 0 or 1
- tail_values: float32 [4608, 128, 128], P(('blk', 'lane')), may hold values from -0.21875 to 0.21875
- tail_reader: int32 [4608], P(('blk', 'lane')), may hold values from 0 to 63, as said below
- tail_target: int32 [4608], P(('blk', 'lane')), may hold values from 0 to 2
Outputs:
- activations: float32 [98304, 512], P(('blk', 'lane'))
The draws below stay inside these ranges and needn't reach their ends.
Inputs may be any that keep to these rules, and one draw needn't show every extreme that they name: `tail_reader`: A tail tile of a device in slab b names a reader (b + o) mod 64 with 1 <= o <= 32; within one device's 18 tail tiles no reader is named more than 1 times, and on every device some reader is named exactly 1 times.
All inputs are finite; a program needn't handle non-finite values. No bound on the sum of `hub_mask` on one device may be relied on, other than what follows from the above.
Results may differ from the reference program's by a relative error of at most 0.0003.
Values sent between devices are 32-bit elements; how exact they have to be, the bound alone decides.
A program may use at most 128 MiB of HBM per device.

```python
import jax
import jax.numpy as jnp
from jax import lax

FEAT = 512
BLOCK = 128
TILES = 6
STOPS = 3
BLOCKS = 3
TAILS = 18
REACH = 32
SLOT_CAP = 1
SLAB = 1536
VERTS = 98304
ALL_TILES = 4608
N_BLK = 64
N_LANE = 4


def draw_tail_reader(key, part):
    special = jax.random.randint(jax.random.fold_in(key, 7), (), 0, N_BLK * N_LANE).astype(jnp.int32)

    def one_device(device_id):
        dev_key = jax.random.fold_in(key, device_id)
        slab_idx = device_id // N_LANE
        hot_offset = jax.random.randint(jax.random.fold_in(dev_key, 1), (), 0, REACH).astype(jnp.int32)
        hot_offset = jnp.where(device_id == special, REACH - 1, hot_offset).astype(jnp.int32)
        others = jax.random.permutation(jax.random.fold_in(dev_key, 2), (REACH - 1) * SLOT_CAP)
        other_offset = (others // SLOT_CAP).astype(jnp.int32)
        other_offset = other_offset + (other_offset >= hot_offset).astype(jnp.int32)
        chosen = jnp.concatenate([jnp.full((SLOT_CAP,), hot_offset, jnp.int32), other_offset[:TAILS - SLOT_CAP]])
        chosen = jax.random.permutation(jax.random.fold_in(dev_key, 3), chosen)
        return ((slab_idx + 1 + chosen) % N_BLK).astype(jnp.int32)
    device_ids = jnp.arange(N_BLK * N_LANE, dtype=jnp.int32)
    return jax.vmap(one_device)(device_ids).reshape(-1).astype(jnp.int32)


def plant(array, key, smallest, top_value):
    spot = [jax.random.randint(jax.random.fold_in(key, axis), (), 0, length) for axis, length in enumerate(array.shape)]
    main_axis = array.shape.index(max(array.shape))
    next_to = spot[:main_axis] + [(spot[main_axis] + 1) % array.shape[main_axis]] + spot[main_axis + 1:]
    return array.at[tuple(spot)].set(smallest).at[tuple(next_to)].set(top_value)


def levels(own_key, shape, cuts, low, top_value):
    level = 1.0
    for position, blocks in cuts:
        heights = jax.random.uniform(jax.random.fold_in(jax.random.fold_in(own_key, 6), position), (blocks,), jnp.float32, low / len(cuts), top_value / len(cuts))
        level = level * jnp.repeat(jnp.exp(heights), shape[position] // blocks).reshape((-1,) + (1,) * (len(shape) - 1 - position))
    return level


def centred(stream_key, extent, deviation, reach, split=(), kind=jnp.bfloat16):
    result = jax.random.normal(stream_key, extent, jnp.float32) * deviation
    if len(split) > 0:
        result = levels(stream_key, extent, split, -0.22, 0.18) * result
    return jnp.clip(result, min=-reach, max=reach).astype(kind)


def setup_inputs(seed: int = 0) -> dict:
    key_of = jax.random.split(jax.random.key(seed), 8)
    features = centred(key_of[0], (VERTS, FEAT), 1.0, 6.0, ((0, 256),), jnp.float32)
    weight = centred(key_of[1], (FEAT, FEAT), FEAT ** -0.5, 0.25, (), jnp.float32)
    hub_values = centred(key_of[2], (STOPS, VERTS, SLAB), (STOPS * SLAB // 2) ** -0.5, 0.125, ((1, 64), (2, 4)), jnp.float32)
    hub_mask = plant((jax.random.randint(key_of[3], (STOPS, VERTS // BLOCK, SLAB // BLOCK), 0, 2) < 1).astype(jnp.int32), jax.random.fold_in(key_of[3], 1), 0, 1)
    tail_values = centred(key_of[4], (ALL_TILES, BLOCK, BLOCK), (BLOCK * TILES) ** -0.5, 0.21875, ((0, 256),), jnp.float32)
    tail_reader = draw_tail_reader(jax.random.fold_in(key_of[7], 71), 0)
    tail_target = plant(jax.random.randint(key_of[6], (ALL_TILES,), 0, BLOCKS), jax.random.fold_in(key_of[6], 1), 0, BLOCKS - 1).astype(jnp.int32)
    return dict(features=features, weight=weight, hub_values=hub_values, hub_mask=hub_mask, tail_values=tail_values, tail_reader=tail_reader, tail_target=tail_target)


def reference(features, weight, hub_values, hub_mask, tail_values, tail_reader, tail_target):
    highest = lax.Precision.HIGHEST
    slabs = features.reshape(N_BLK, SLAB, FEAT)
    tile_rows = SLAB // BLOCK

    def one_slab(slab_idx):
        running = jnp.zeros((SLAB, FEAT), jnp.float32)
        for stop_idx in range(STOPS):
            hub_slice = lax.dynamic_slice_in_dim(hub_values[stop_idx], slab_idx * SLAB, SLAB, 0)
            mask_slice = lax.dynamic_slice_in_dim(hub_mask[stop_idx], slab_idx * tile_rows, tile_rows, 0)
            expanded = jnp.repeat(jnp.repeat(mask_slice.astype(jnp.float32), BLOCK, 0), BLOCK, 1)
            source = slabs[(slab_idx - stop_idx) % N_BLK]
            running = running + jnp.dot(hub_slice * expanded, source, precision=highest, preferred_element_type=jnp.float32)
        return running

    hub_agg = lax.map(one_slab, jnp.arange(N_BLK, dtype=jnp.int32)).reshape(VERTS, FEAT)

    device_total = N_BLK * N_LANE
    block_feats = features.reshape(device_total, BLOCKS, BLOCK, FEAT)
    tile_vals = tail_values.reshape(device_total, BLOCKS, TILES, BLOCK, BLOCK)

    def device_products(pair):
        return jnp.einsum("kjab,kbf->kjaf", pair[0], pair[1], precision=highest)

    products = lax.map(device_products, (tile_vals, block_feats))
    device_ids = jnp.arange(device_total, dtype=jnp.int32)[:, None]
    lane_ids = device_ids % N_LANE
    readers = tail_reader.reshape(device_total, TAILS)
    targets = tail_target.reshape(device_total, TAILS)
    dest_block = ((readers * N_LANE + lane_ids) * BLOCKS + targets).astype(jnp.int32)
    tail_agg = jax.ops.segment_sum(products.reshape(-1, BLOCK, FEAT), dest_block.reshape(-1), num_segments=device_total * BLOCKS)
    combined = hub_agg + tail_agg.reshape(VERTS, FEAT)
    return jnp.maximum(jnp.dot(combined, weight, precision=highest, preferred_element_type=jnp.float32), 0.0)
```

```python
import functools

import jax
import jax.numpy as jnp
from jax import lax
from jax.experimental import pallas as pl
from jax.experimental.pallas import tpu as pltpu
from jax.sharding import PartitionSpec as P

MESH = pl.DeviceIdType.MESH
BLOCK = 128
TILES = 6
TAILS = 18
NZ, NX, NY = 8, 4, 2
PLANE = NX * NY
WIN = 4
ROWS, FEAT = 384, 512
NC = 4
N = FEAT // NC
SPLIT = 192
BF = jnp.bfloat16
F32 = jnp.float32


def halves(value):
    hi = value.astype(BF)
    return hi, (value - hi.astype(F32)).astype(BF)


def dot3(ah, al, bh, bl):
    def dot(a, b):
        return jnp.dot(a, b, preferred_element_type=F32)

    return dot(ah, bh) + (dot(ah, bl) + dot(al, bh))


def kernel(
    feat_hbm, weight_hbm, hub_hbm, tail_hbm, mask, slot_tile, meta,
    out,
    fbuf, fh, fl, tsend, trecv, tvals, mrecv, mscal, eh, el, rh, rl, hubv, ah, al, hh, hl,
    run, crecv, hrecv, acc, zrecv, wv, wh, wl,
    load_sem, gs, gr, ts, tr, ms, mr, cs, cr, hs, hr, zs, zr, ws, wr,
):
    blk, lane = lax.axis_index("blk"), lax.axis_index("lane")
    z, p = lax.div(blk, PLANE), lax.rem(blk, PLANE)
    x, y = lax.div(p, NY), lax.rem(p, NY)
    h, c = lax.div(lane, 2), lax.rem(lane, 2)

    def at(zz, pp, hh_=None, cc=None):
        hh_ = h if hh_ is None else hh_
        cc = c if cc is None else cc
        return {"blk": lax.rem(zz + NZ, NZ) * PLANE + pp, "lane": hh_ * 2 + cc}

    def pos(xx, yy):
        return lax.rem(xx + NX, NX) * NY + yy

    def remote(src, dst, send, recv, dev):
        return pltpu.make_async_remote_copy(
            src_ref=src, dst_ref=dst, send_sem=send, recv_sem=recv, device_id=dev, device_id_type=MESH
        )

    feat_in = [
        pltpu.make_async_copy(feat_hbm.at[:, pl.ds(n * N, N)], fbuf.at[n, p], load_sem.at[n]) for n in range(NC)
    ]
    tail_in = pltpu.make_async_copy(tail_hbm, tvals.at[pl.ds(0, TAILS)], load_sem.at[NC])
    hub_in = [pltpu.make_async_copy(hub_hbm.at[s], hubv.at[s], load_sem.at[NC + 1 + s]) for s in range(3)]
    weight_in = pltpu.make_async_copy(weight_hbm, wv, load_sem.at[NC + 4])
    meta_in = pltpu.make_async_copy(meta.at[p], mrecv.at[p], load_sem.at[NC + 5])
    feat_in[0].start()
    tail_in.start()
    meta_in.start()
    for copy in feat_in[1:] + hub_in + [weight_in]:
        copy.start()

    barrier = pltpu.get_barrier_semaphore()
    partners = [at(z, lax.rem(p + i, PLANE)) for i in range(1, PLANE)]
    partners += [at(z + 1, p), at(z - 1, p), at(z + 4, p), at(z, p, h, 1 - c), at(z, p, 1 - h, c)]
    for dev in partners:
        pl.semaphore_signal(barrier, inc=1, device_id=dev, device_id_type=MESH)
    pl.semaphore_wait(barrier, len(partners))

    yn, left, right = pos(x, 1 - y), pos(x - 1, y), pos(x + 1, y)
    right_yn = pos(x + 1, 1 - y)
    flows = [(p, yn), (p, right), (p, left), (yn, right), (yn, left), (left, right), (right_yn, left)]

    def gather(n, i):
        slot, dest = flows[i]
        return remote(fbuf.at[n, slot], fbuf.at[n, slot], gs.at[n, i], gr.at[n, i], at(z, dest))

    gathers = [[gather(n, i) for i in range(7)] for n in range(NC)]

    def first_sends(n):
        feat_in[n].wait()
        for i in range(3):
            gathers[n][i].start()

    wraps = [
        [
            remote(fbuf.at[n, 7 - i], fbuf.at[n, 8 + i], ws.at[n, i], wr.at[n, i], at(z + 1, p))
            for i in range(2)
        ]
        for n in range(NC)
    ]

    first_sends(0)

    tail_in.wait()
    tvals[TAILS] = jnp.zeros((BLOCK, BLOCK), F32)
    tile_copies, meta_copies = [], []
    for i in range(1, PLANE):
        q = lax.rem(p + i, PLANE)
        for j in range(WIN):
            tsend[q, j] = tvals[slot_tile[q * WIN + j]]
        tile_copies.append(remote(tsend.at[q], trecv.at[p], ts.at[i - 1], tr.at[i - 1], at(z, q)))
        meta_copies.append(remote(meta.at[q], mrecv.at[p], ms.at[i - 1], mr.at[i - 1], at(z, q)))
        tile_copies[-1].start()
        meta_copies[-1].start()
    for j in range(WIN):
        trecv[p, j] = tvals[slot_tile[p * WIN + j]]

    first_sends(1)

    for s in range(3):
        hub_in[s].wait()

        def hub_rows(i, carry):
            for jj in range(3):
                present = mask[s, i, jj].astype(F32)
                rows = pl.ds(pl.multiple_of(i * BLOCK, BLOCK), BLOCK)
                hi, lo = halves(hubv[s, rows, jj * BLOCK:(jj + 1) * BLOCK] * present)
                cols = slice(s * ROWS + jj * BLOCK, s * ROWS + (jj + 1) * BLOCK)
                ah[rows, cols] = hi
                al[rows, cols] = lo
            return carry

        lax.fori_loop(0, 12, hub_rows, 0)
    weight_in.wait()
    for i in range(4):
        hi, lo = halves(wv[i * BLOCK:(i + 1) * BLOCK])
        wh[i * BLOCK:(i + 1) * BLOCK] = hi
        wl[i * BLOCK:(i + 1) * BLOCK] = lo

    order = ([4, 3, 2, 1], [1, 2, 3, 4])
    part = (slice(0, SPLIT), slice(SPLIT, ROWS))
    size = (SPLIT, ROWS - SPLIT)

    def chain(n, way, s):
        rows = pl.ds(0, size[way])
        src = acc.at[n, order[way][0], pl.ds(part[way].start, size[way])] if s == 0 else zrecv.at[n, way, s - 1, rows]
        zz = z + 1 if way == 0 else (z - 1 if s < 3 else z + 4)
        return remote(src, zrecv.at[n, way, s, rows], zs.at[n, way, s], zr.at[n, way, s], at(zz, p))

    chains = [[[chain(n, way, s) for s in range(4)] for way in range(2)] for n in range(NC)]

    def chain_step(n, s):
        for way in range(2):
            chains[n][way][s - 1].wait_recv()
            rows = slice(0, size[way])
            zrecv[n, way, s - 1, rows] = zrecv[n, way, s - 1, rows] + acc[n, order[way][s], part[way]]
            chains[n][way][s].start()

    def tail_product(n, d):
        for pp in range(PLANE):
            j = d - (p <= pp).astype(jnp.int32)
            k = mscal[pp, 0, jnp.clip(j, 0, WIN - 1)] + 3 * pp
            rh[pp * BLOCK:(pp + 1) * BLOCK] = fh[k]
            rl[pp * BLOCK:(pp + 1) * BLOCK] = fl[k]
        acc[n, d] = dot3(eh[d], el[d], rh[...], rl[...])

    def convert(n, slot):
        for i in range(3):
            hi, lo = halves(fbuf[n, slot, i * BLOCK:(i + 1) * BLOCK])
            fh[slot * 3 + i] = hi
            fl[slot * 3 + i] = lo

    slot1 = jnp.where(p >= 1, p - 1, 8)
    slot2 = jnp.where(p >= 2, p - 2, jnp.where(p == 1, 8, 9))

    core_copies = [
        remote(run.at[n, 1 - c], crecv.at[n], cs.at[n], cr.at[n], at(z, p, h, 1 - c)) for n in range(NC)
    ]
    half_rows = (pl.ds(0, ROWS // 2), pl.ds(ROWS // 2, ROWS // 2))
    half_copies = [
        [
            remote(run.at[n, c, 1 - h, half_rows[i]], hrecv.at[n, half_rows[i]], hs.at[n, i], hr.at[n, i], at(z, p, 1 - h, c))
            for i in range(2)
        ]
        for n in range(NC)
    ]

    def hub_product(n):
        for s, slot in enumerate((p, slot1, slot2)):
            for i in range(3):
                rows = slice(s * ROWS + i * BLOCK, s * ROWS + (i + 1) * BLOCK)
                hh[rows] = fh[slot * 3 + i]
                hl[rows] = fl[slot * 3 + i]

        def quarter(i, carry):
            rows = pl.ds(pl.multiple_of(i * ROWS, BLOCK), ROWS)
            run[n, lax.rem(i, 2), lax.div(i, 2)] = dot3(ah[rows], al[rows], hh[...], hl[...])
            return carry

        lax.fori_loop(0, 4, quarter, 0)
        core_copies[n].start()

    def hub_sum(n):
        core_copies[n].wait_recv()
        for i in range(2):
            run[n, c, i] = run[n, c, i] + crecv[n, i]
        for copy in half_copies[n]:
            copy.start()

    def finish(n):
        for way in range(2):
            chains[n][way][3].wait_recv()
        for copy in half_copies[n]:
            copy.wait_recv()
        for way in range(2):
            rows = part[way]
            total = (run[n, c, h, rows] + hrecv[n, rows]) + (acc[n, 0, rows] + zrecv[n, way, 3, 0:size[way]])
            hi, lo = halves(total)
            cols = slice(n * N, (n + 1) * N)
            value = dot3(hi, lo, wh[cols], wl[cols])
            if n > 0:
                value = out[rows] + value
            out[rows] = jnp.maximum(value, 0.0) if n == NC - 1 else value

    def build_tiles():
        meta_in.wait()
        for copy in meta_copies:
            copy.wait_recv()
        scal = pltpu.make_async_copy(mrecv, mscal, load_sem.at[NC + 6])
        scal.start()
        for copy in tile_copies:
            copy.wait_recv()
        scal.wait()

        def source(pp, carry):
            cols = pl.ds(pl.multiple_of(pp * BLOCK, BLOCK), BLOCK)
            none = pl.ds(0, ROWS)
            zero = jnp.zeros((ROWS, BLOCK), BF)
            empty = jnp.where(pp < p, 4, 0)
            eh[empty, none, cols] = zero
            el[empty, none, cols] = zero
            for j in range(WIN):
                d = j + (p <= pp).astype(jnp.int32)
                value = trecv[pp, j]
                target = mscal[pp, 1, j]
                for t in range(3):
                    hi, lo = halves(value * (target == t).astype(F32))
                    eh[d, t * BLOCK:(t + 1) * BLOCK, cols] = hi
                    el[d, t * BLOCK:(t + 1) * BLOCK, cols] = lo
            return carry

        lax.fori_loop(0, PLANE, source, 0)

    pending = []

    def serve(count=1):
        for _ in range(count):
            if pending:
                chain_step(*pending.pop(0))

    for n in range(NC):
        g = gathers[n]
        g[0].wait_recv()
        g[3].start()
        g[4].start()
        g[1].wait_recv()
        g[5].start()
        g[4].wait_recv()
        g[6].start()
        if n + 2 < NC:
            first_sends(n + 2)
        if n == 0:
            build_tiles()
        else:
            hub_sum(n - 1)
        serve()
        for i in (2, 3, 5, 6):
            g[i].wait_recv()
        for i in range(2):

            @pl.when(p < 2 - i)
            def _():
                wraps[n][i].start()

        lax.fori_loop(0, PLANE, lambda slot, carry: (convert(n, slot), carry)[1], 0)
        tail_product(n, 4)
        chains[n][0][0].start()
        tail_product(n, 1)
        chains[n][1][0].start()
        serve()
        tail_product(n, 3)
        tail_product(n, 2)
        serve()
        tail_product(n, 0)
        for i in range(2):

            @pl.when(p < 2 - i)
            def _():
                wraps[n][i].wait_recv()
                convert(n, 8 + i)

        hub_product(n)
        if n > 0:
            finish_before = n - 1
            while pending and pending[0][0] < finish_before:
                serve()
        pending.extend((n, s) for s in range(1, 4))

    hub_sum(NC - 1)
    done = 0
    while pending:
        step = pending[0]
        while done < step[0]:
            finish(done)
            done += 1
        serve()
    while done < NC:
        finish(done)
        done += 1

    for n in range(NC):
        for copy in gathers[n]:
            copy.wait_send()
        for way in range(2):
            for copy in chains[n][way]:
                copy.wait_send()
        core_copies[n].wait_send()
        for copy in half_copies[n]:
            copy.wait_send()
        for i in range(2):

            @pl.when(p < 2 - i)
            def _():
                wraps[n][i].wait_send()
    for copy in tile_copies + meta_copies:
        copy.wait_send()


def slot_tables(tail_reader, tail_target):
    blk = lax.axis_index("blk")
    z, p = blk // PLANE, blk % PLANE
    q = jnp.arange(PLANE * WIN, dtype=jnp.int32) // WIN
    j = jnp.arange(PLANE * WIN, dtype=jnp.int32) % WIN
    reader = ((z + j + (q <= p)) % NZ) * PLANE + q
    found = (tail_reader[None, :] == reader[:, None]).astype(jnp.int32)
    tiles = jnp.arange(TAILS, dtype=jnp.int32)
    tile = jnp.sum(found * (tiles - TAILS)[None, :], 1) + TAILS
    source = jnp.sum(found * (tiles // TILES)[None, :], 1)
    target = jnp.sum(found * tail_target[None, :], 1)
    meta = jnp.stack([source.reshape(PLANE, WIN), target.reshape(PLANE, WIN)], 1)
    meta = jnp.pad(meta, ((0, 0), (0, 6), (0, BLOCK - WIN)))
    return tile, meta


def per_device(features, weight, hub_values, hub_mask, tail_values, tail_reader, tail_target):
    tile, meta = slot_tables(tail_reader, tail_target)
    dma = pltpu.SemaphoreType.DMA
    any_ = pl.BlockSpec(memory_space=pl.ANY)
    vmem = pl.BlockSpec(memory_space=pltpu.VMEM)
    smem = pl.BlockSpec(memory_space=pltpu.SMEM)
    return pl.pallas_call(
        kernel,
        out_shape=jax.ShapeDtypeStruct((ROWS, FEAT), F32),
        in_specs=[any_, any_, any_, any_, smem, smem, vmem],
        out_specs=vmem,
        scratch_shapes=[
            pltpu.VMEM((NC, 10, ROWS, N), F32),
            pltpu.VMEM((30, BLOCK, N), BF),
            pltpu.VMEM((30, BLOCK, N), BF),
            pltpu.VMEM((PLANE, WIN, BLOCK, BLOCK), F32),
            pltpu.VMEM((PLANE, WIN, BLOCK, BLOCK), F32),
            pltpu.VMEM((TAILS + 1, BLOCK, BLOCK), F32),
            pltpu.VMEM((PLANE, 8, BLOCK), jnp.int32),
            pltpu.SMEM((PLANE, 8, BLOCK), jnp.int32),
            pltpu.VMEM((5, ROWS, PLANE * BLOCK), BF),
            pltpu.VMEM((5, ROWS, PLANE * BLOCK), BF),
            pltpu.VMEM((PLANE * BLOCK, N), BF),
            pltpu.VMEM((PLANE * BLOCK, N), BF),
            pltpu.VMEM((3, 4 * ROWS, ROWS), F32),
            pltpu.VMEM((4 * ROWS, 3 * ROWS), BF),
            pltpu.VMEM((4 * ROWS, 3 * ROWS), BF),
            pltpu.VMEM((3 * ROWS, N), BF),
            pltpu.VMEM((3 * ROWS, N), BF),
            pltpu.VMEM((NC, 2, 2, ROWS, N), F32),
            pltpu.VMEM((NC, 2, ROWS, N), F32),
            pltpu.VMEM((NC, ROWS, N), F32),
            pltpu.VMEM((NC, 5, ROWS, N), F32),
            pltpu.VMEM((NC, 2, 4, max(SPLIT, ROWS - SPLIT), N), F32),
            pltpu.VMEM((FEAT, FEAT), F32),
            pltpu.VMEM((FEAT, FEAT), BF),
            pltpu.VMEM((FEAT, FEAT), BF),
            dma((NC + 7,)),
            dma((NC, 7)),
            dma((NC, 7)),
            dma((7,)),
            dma((7,)),
            dma((7,)),
            dma((7,)),
            dma((NC,)),
            dma((NC,)),
            dma((NC, 2)),
            dma((NC, 2)),
            dma((NC, 2, 4)),
            dma((NC, 2, 4)),
            dma((NC, 2)),
            dma((NC, 2)),
        ],
        compiler_params=pltpu.CompilerParams(
            collective_id=0, has_side_effects=True, vmem_limit_bytes=62 << 20
        ),
    )(features, weight, hub_values, tail_values, hub_mask, tile, meta)


def solution(mesh):
    return jax.shard_map(
        per_device,
        mesh=mesh,
        in_specs=(
            P(("blk", "lane"), None),
            P(),
            P(None, "blk", "lane"),
            P(None, "blk", "lane"),
            P(("blk", "lane"), None, None),
            P(("blk", "lane")),
            P(("blk", "lane")),
        ),
        out_specs=P(("blk", "lane"), None),
        check_vma=False,
    )
```

```python
import functools

import jax
import jax.numpy as jnp
from jax import lax
from jax.experimental import pallas as pl
from jax.experimental.pallas import tpu as pltpu
from jax.sharding import PartitionSpec as P

MESH = pl.DeviceIdType.MESH
BLOCK = 128
TILES = 6
TAILS = 18
NZ, NX, NY = 8, 4, 2
PLANE = NX * NY
WIN = 4
ROWS, FEAT = 384, 512
NC = 4
N = FEAT // NC
SPLIT = 128
BF = jnp.bfloat16
F32 = jnp.float32


def halves(value):
    hi = value.astype(BF)
    return hi, (value - hi.astype(F32)).astype(BF)


def dot3(ah, al, bh, bl):
    def dot(a, b):
        return jnp.dot(a, b, preferred_element_type=F32)

    return dot(ah, bh) + (dot(ah, bl) + dot(al, bh))


def dot_pair(ah, al, pair):
    both = jnp.dot(ah, pair, preferred_element_type=F32)
    return (both[:, :N] + both[:, N:]) + jnp.dot(al, pair[:, :N], preferred_element_type=F32)


def kernel(
    feat_hbm, weight_hbm, hub_hbm, tail_hbm, mask, slot_tile, meta,
    out,
    fbuf, fpair, tsend, tmid, trecv, tvals, mrecv, mscal, eh, el, rpair, hubv, ah, al, hpair,
    run, crecv, hrecv, acc, zrecv, wv, wh, wl,
    load_sem, gs, gr, ts, tr, ms, mr, cs, cr, hs, hr, zs, zr, ws, wr,
):
    blk, lane = lax.axis_index("blk"), lax.axis_index("lane")
    z, p = lax.div(blk, PLANE), lax.rem(blk, PLANE)
    x, y = lax.div(p, NY), lax.rem(p, NY)
    h, c = lax.div(lane, 2), lax.rem(lane, 2)

    def at(zz, pp, hh_=None, cc=None):
        hh_ = h if hh_ is None else hh_
        cc = c if cc is None else cc
        return {"blk": lax.rem(zz + NZ, NZ) * PLANE + pp, "lane": hh_ * 2 + cc}

    def pos(xx, yy):
        return lax.rem(xx + NX, NX) * NY + yy

    def remote(src, dst, send, recv, dev):
        return pltpu.make_async_remote_copy(
            src_ref=src, dst_ref=dst, send_sem=send, recv_sem=recv, device_id=dev, device_id_type=MESH
        )

    feat_in = [
        pltpu.make_async_copy(feat_hbm.at[:, pl.ds(n * N, N)], fbuf.at[n, p], load_sem.at[n]) for n in range(NC)
    ]
    tail_in = pltpu.make_async_copy(tail_hbm, tvals.at[pl.ds(0, TAILS)], load_sem.at[NC])
    hub_in = [pltpu.make_async_copy(hub_hbm.at[s], hubv.at[s], load_sem.at[NC + 1 + s]) for s in range(3)]
    weight_in = pltpu.make_async_copy(weight_hbm, wv, load_sem.at[NC + 4])
    meta_in = pltpu.make_async_copy(meta.at[p], mrecv.at[p], load_sem.at[NC + 5])
    feat_in[0].start()
    tail_in.start()
    meta_in.start()
    for copy in feat_in[1:] + hub_in + [weight_in]:
        copy.start()

    barrier = pltpu.get_barrier_semaphore()
    partners = [at(z, lax.rem(p + i, PLANE)) for i in range(1, PLANE)]
    partners += [at(z + 1, p), at(z - 1, p), at(z + 4, p), at(z, p, h, 1 - c), at(z, p, 1 - h, c)]
    for dev in partners:
        pl.semaphore_signal(barrier, inc=1, device_id=dev, device_id_type=MESH)
    pl.semaphore_wait(barrier, len(partners))

    yn, left, right = pos(x, 1 - y), pos(x - 1, y), pos(x + 1, y)
    right_yn = pos(x + 1, 1 - y)
    flows = [(p, yn), (p, right), (p, left), (yn, right), (yn, left), (left, right), (right_yn, left)]

    def gather(n, i):
        slot, dest = flows[i]
        return remote(fbuf.at[n, slot], fbuf.at[n, slot], gs.at[n, i], gr.at[n, i], at(z, dest))

    gathers = [[gather(n, i) for i in range(7)] for n in range(NC)]

    def first_sends(n):
        feat_in[n].wait()
        for i in range(3):
            gathers[n][i].start()

    wraps = [
        remote(fbuf.at[n, 6 + y], fbuf.at[n, 9 - y], ws.at[n, 0], wr.at[n, 0], at(z + 1, p)) for n in range(NC)
    ]
    wraps_on = [remote(fbuf.at[n, 8], fbuf.at[n, 8], ws.at[n, 1], wr.at[n, 1], at(z, yn)) for n in range(NC)]

    first_sends(0)

    tail_in.wait()
    tvals[TAILS] = jnp.zeros((BLOCK, BLOCK), F32)
    meta_copies = []
    for i in range(1, PLANE):
        q = lax.rem(p + i, PLANE)
        meta_copies.append(remote(meta.at[q], mrecv.at[p], ms.at[i - 1], mr.at[i - 1], at(z, q)))
        meta_copies[-1].start()
    steps = (1, 3, 2)
    cross, direct, onward = [], [], []

    def fill(q):
        for j in range(WIN):
            tsend[q, j] = tvals[slot_tile[q * WIN + j]]

    for i, dx in enumerate(steps + (0,)):
        q = pos(x + dx, 1 - y)
        fill(q)
        landing = tmid.at[lax.rem(x + dx, NX)] if dx else trecv.at[p]
        cross.append(remote(tsend.at[q], landing, ts.at[0, i], tr.at[0, i], at(z, yn)))
        cross[-1].start()
    for i, dx in enumerate(steps):
        q = pos(x + dx, y)
        fill(q)
        direct.append(remote(tsend.at[q], trecv.at[p], ts.at[1, i], tr.at[1, i], at(z, q)))
        direct[-1].start()
        onward.append(remote(tmid.at[lax.rem(x + dx, NX)], trecv.at[yn], ts.at[2, i], tr.at[2, i], at(z, q)))

    def pass_tile(i):
        cross[i].wait_recv()
        onward[i].start()

    for j in range(WIN):
        trecv[p, j] = tvals[slot_tile[p * WIN + j]]

    def wrap_send(n):
        @pl.when(p < 2)
        def _():
            wraps[n].start()

    def wrap_forward(n):
        @pl.when(p == 1)
        def _():
            wraps[n].wait_recv()
            wraps_on[n].start()

    def second_sends(n):
        gathers[n][0].wait_recv()
        gathers[n][3].start()
        gathers[n][4].start()
        gathers[n][1].wait_recv()
        wrap_send(n)
        gathers[n][5].start()

    def third_send(n):
        gathers[n][4].wait_recv()
        gathers[n][6].start()

    def hub_tiles(s):
        hub_in[s].wait()

        def hub_rows(i, carry):
            for jj in range(3):
                present = mask[s, i, jj].astype(F32)
                rows = pl.ds(pl.multiple_of(i * BLOCK, BLOCK), BLOCK)
                hi, lo = halves(hubv[s, rows, jj * BLOCK:(jj + 1) * BLOCK] * present)
                cols = slice(s * ROWS + jj * BLOCK, s * ROWS + (jj + 1) * BLOCK)
                ah[rows, cols] = hi
                al[rows, cols] = lo
            return carry

        lax.fori_loop(0, 12, hub_rows, 0)

    second_sends(0)
    hub_tiles(0)
    pass_tile(0)
    third_send(0)
    first_sends(1)
    hub_tiles(1)
    pass_tile(1)
    hub_tiles(2)
    pass_tile(2)
    wrap_forward(0)
    weight_in.wait()
    for i in range(4):
        hi, lo = halves(wv[i * BLOCK:(i + 1) * BLOCK])
        wh[i * BLOCK:(i + 1) * BLOCK] = hi
        wl[i * BLOCK:(i + 1) * BLOCK] = lo

    order = ([4, 3, 2, 1], [1, 2, 3, 4])
    part = (slice(0, SPLIT), slice(SPLIT, ROWS))
    size = (SPLIT, ROWS - SPLIT)

    def chain(n, way, s):
        rows = pl.ds(0, size[way])
        src = acc.at[n, order[way][0], pl.ds(part[way].start, size[way])] if s == 0 else zrecv.at[n, way, s - 1, rows]
        zz = z + 1 if way == 0 else (z - 1 if s < 3 else z + 4)
        return remote(src, zrecv.at[n, way, s, rows], zs.at[n, way, s], zr.at[n, way, s], at(zz, p))

    chains = [[[chain(n, way, s) for s in range(4)] for way in range(2)] for n in range(NC)]

    def chain_step(n, s):
        for way in range(2):
            chains[n][way][s - 1].wait_recv()
            rows = slice(0, size[way])
            zrecv[n, way, s - 1, rows] = zrecv[n, way, s - 1, rows] + acc[n, order[way][s], part[way]]
            chains[n][way][s].start()

    def tail_product(n, d):
        for pp in range(PLANE):
            j = d - (p <= pp).astype(jnp.int32)
            k = mscal[pp, 0, jnp.clip(j, 0, WIN - 1)] + 3 * pp
            rpair[pp * BLOCK:(pp + 1) * BLOCK] = fpair[k]
        acc[n, d] = dot_pair(eh[d], el[d], rpair[...])

    def convert(n):
        def one(slot, carry):
            for i in range(3):
                hi, lo = halves(fbuf[n, slot, i * BLOCK:(i + 1) * BLOCK])
                fpair[slot * 3 + i, :, :N] = hi
                fpair[slot * 3 + i, :, N:] = lo
            return carry

        lax.fori_loop(0, PLANE, one, 0)

    def hub_fill(n):
        for s in range(3):
            slot = jnp.maximum(p - s, 0)
            for i in range(3):
                hpair[s * ROWS + i * BLOCK:s * ROWS + (i + 1) * BLOCK] = fpair[slot * 3 + i]

    def hub_fill_wrap(n):
        def put(s, slot):
            hi, lo = halves(fbuf[n, slot])
            hpair[s * ROWS:(s + 1) * ROWS, :N] = hi
            hpair[s * ROWS:(s + 1) * ROWS, N:] = lo

        @pl.when(p == 0)
        def _():
            wraps_on[n].wait_recv()
            put(1, 8)
            wraps[n].wait_recv()
            put(2, 9)

        @pl.when(p == 1)
        def _():
            put(2, 8)

    core_copies = [
        remote(run.at[n, 1 - c], crecv.at[n], cs.at[n], cr.at[n], at(z, p, h, 1 - c)) for n in range(NC)
    ]
    half_rows = (pl.ds(0, ROWS // 2), pl.ds(ROWS // 2, ROWS // 2))
    half_copies = [
        [
            remote(run.at[n, c, 1 - h, half_rows[i]], hrecv.at[n, half_rows[i]], hs.at[n, i], hr.at[n, i], at(z, p, 1 - h, c))
            for i in range(2)
        ]
        for n in range(NC)
    ]

    def hub_product(n):
        def quarter(i, carry):
            rows = pl.ds(pl.multiple_of(i * ROWS, BLOCK), ROWS)
            run[n, lax.rem(i, 2), lax.div(i, 2)] = dot_pair(ah[rows], al[rows], hpair[...])
            return carry

        lax.fori_loop(0, 4, quarter, 0)
        core_copies[n].start()

    def hub_sum(n):
        core_copies[n].wait_recv()
        for i in range(2):
            run[n, c, i] = run[n, c, i] + crecv[n, i]
        for copy in half_copies[n]:
            copy.start()

    def finish(n):
        for way in range(2):
            chains[n][way][3].wait_recv()
        for copy in half_copies[n]:
            copy.wait_recv()
        for way in range(2):
            rows = part[way]
            total = (run[n, c, h, rows] + hrecv[n, rows]) + (acc[n, 0, rows] + zrecv[n, way, 3, 0:size[way]])
            hi, lo = halves(total)
            cols = slice(n * N, (n + 1) * N)
            value = dot3(hi, lo, wh[cols], wl[cols])
            if n > 0:
                value = out[rows] + value
            out[rows] = jnp.maximum(value, 0.0) if n == NC - 1 else value

    def build_tile(pp):
        cols = pl.ds(pl.multiple_of(pp * BLOCK, BLOCK), BLOCK)
        zero = jnp.zeros((ROWS, BLOCK), BF)
        empty = jnp.where(pp < p, 4, 0)
        eh[empty, pl.ds(0, ROWS), cols] = zero
        el[empty, pl.ds(0, ROWS), cols] = zero
        for j in range(WIN):
            d = j + (p <= pp).astype(jnp.int32)
            value = trecv[pp, j]
            target = mscal[pp, 1, j]
            hi = value.astype(BF).astype(F32)
            lo = value - hi
            for t in range(3):
                keep = (target == t).astype(F32)
                eh[d, t * BLOCK:(t + 1) * BLOCK, cols] = (hi * keep).astype(BF)
                el[d, t * BLOCK:(t + 1) * BLOCK, cols] = (lo * keep).astype(BF)

    meta_in.wait()
    for copy in meta_copies:
        copy.wait_recv()
    scal = pltpu.make_async_copy(mrecv, mscal, load_sem.at[NC + 6])
    scal.start()
    scal.wait()
    build_tile(p)
    for i, dx in enumerate(steps):
        direct[i].wait_recv()
        build_tile(pos(x - dx, y))
    cross[3].wait_recv()
    build_tile(yn)
    second_sends(1)
    for i, dx in enumerate(steps):
        onward[i].wait_recv()
        build_tile(pos(x - dx, 1 - y))

    for n in range(NC):
        if n > 0 and n + 1 < NC:
            second_sends(n + 1)
        if n + 2 < NC:
            first_sends(n + 2)
        for i in (2, 3, 5, 6):
            gathers[n][i].wait_recv()
        if n > 0:
            chain_step(n - 1, 2)
        if n + 1 < NC:
            third_send(n + 1)
        convert(n)
        tail_product(n, 4)
        chains[n][0][0].start()
        tail_product(n, 1)
        chains[n][1][0].start()
        if n > 0:
            chain_step(n - 1, 3)
        hub_fill(n)
        hub_fill_wrap(n)
        hub_product(n)
        tail_product(n, 3)
        tail_product(n, 2)
        chain_step(n, 1)
        tail_product(n, 0)
        if n + 1 < NC:
            wrap_forward(n + 1)
        hub_sum(n)
        if n > 0:
            finish(n - 1)

    last = NC - 1
    chain_step(last, 2)
    chain_step(last, 3)
    finish(last)

    for n in range(NC):
        for copy in gathers[n]:
            copy.wait_send()
        for way in range(2):
            for copy in chains[n][way]:
                copy.wait_send()
        core_copies[n].wait_send()
        for copy in half_copies[n]:
            copy.wait_send()

        @pl.when(p < 2)
        def _():
            wraps[n].wait_send()

        @pl.when(p == 1)
        def _():
            wraps_on[n].wait_send()

    for copy in cross + direct + onward + meta_copies:
        copy.wait_send()


def slot_tables(tail_reader, tail_target):
    blk = lax.axis_index("blk")
    z, p = blk // PLANE, blk % PLANE
    q = jnp.arange(PLANE * WIN, dtype=jnp.int32) // WIN
    j = jnp.arange(PLANE * WIN, dtype=jnp.int32) % WIN
    reader = ((z + j + (q <= p)) % NZ) * PLANE + q
    found = (tail_reader[None, :] == reader[:, None]).astype(jnp.int32)
    tiles = jnp.arange(TAILS, dtype=jnp.int32)
    tile = jnp.sum(found * (tiles - TAILS)[None, :], 1) + TAILS
    source = jnp.sum(found * (tiles // TILES)[None, :], 1)
    target = jnp.sum(found * tail_target[None, :], 1)
    meta = jnp.stack([source.reshape(PLANE, WIN), target.reshape(PLANE, WIN)], 1)
    meta = jnp.pad(meta, ((0, 0), (0, 6), (0, BLOCK - WIN)))
    return tile, meta


def per_device(features, weight, hub_values, hub_mask, tail_values, tail_reader, tail_target):
    tile, meta = slot_tables(tail_reader, tail_target)
    dma = pltpu.SemaphoreType.DMA
    any_ = pl.BlockSpec(memory_space=pl.ANY)
    vmem = pl.BlockSpec(memory_space=pltpu.VMEM)
    smem = pl.BlockSpec(memory_space=pltpu.SMEM)
    return pl.pallas_call(
        kernel,
        out_shape=jax.ShapeDtypeStruct((ROWS, FEAT), F32),
        in_specs=[any_, any_, any_, any_, smem, smem, vmem],
        out_specs=vmem,
        scratch_shapes=[
            pltpu.VMEM((NC, 10, ROWS, N), F32),
            pltpu.VMEM((24, BLOCK, 2 * N), BF),
            pltpu.VMEM((PLANE, WIN, BLOCK, BLOCK), F32),
            pltpu.VMEM((NX, WIN, BLOCK, BLOCK), F32),
            pltpu.VMEM((PLANE, WIN, BLOCK, BLOCK), F32),
            pltpu.VMEM((TAILS + 1, BLOCK, BLOCK), F32),
            pltpu.VMEM((PLANE, 8, BLOCK), jnp.int32),
            pltpu.SMEM((PLANE, 8, BLOCK), jnp.int32),
            pltpu.VMEM((5, ROWS, PLANE * BLOCK), BF),
            pltpu.VMEM((5, ROWS, PLANE * BLOCK), BF),
            pltpu.VMEM((PLANE * BLOCK, 2 * N), BF),
            pltpu.VMEM((3, 4 * ROWS, ROWS), F32),
            pltpu.VMEM((4 * ROWS, 3 * ROWS), BF),
            pltpu.VMEM((4 * ROWS, 3 * ROWS), BF),
            pltpu.VMEM((3 * ROWS, 2 * N), BF),
            pltpu.VMEM((NC, 2, 2, ROWS, N), F32),
            pltpu.VMEM((NC, 2, ROWS, N), F32),
            pltpu.VMEM((NC, ROWS, N), F32),
            pltpu.VMEM((NC, 5, ROWS, N), F32),
            pltpu.VMEM((NC, 2, 4, max(SPLIT, ROWS - SPLIT), N), F32),
            pltpu.VMEM((FEAT, FEAT), F32),
            pltpu.VMEM((FEAT, FEAT), BF),
            pltpu.VMEM((FEAT, FEAT), BF),
            dma((NC + 7,)),
            dma((NC, 7)),
            dma((NC, 7)),
            dma((3, 4)),
            dma((3, 4)),
            dma((7,)),
            dma((7,)),
            dma((NC,)),
            dma((NC,)),
            dma((NC, 2)),
            dma((NC, 2)),
            dma((NC, 2, 4)),
            dma((NC, 2, 4)),
            dma((NC, 2)),
            dma((NC, 2)),
        ],
        compiler_params=pltpu.CompilerParams(
            collective_id=0, has_side_effects=True, vmem_limit_bytes=62 << 20
        ),
    )(features, weight, hub_values, tail_values, hub_mask, tile, meta)


def solution(mesh):
    return jax.shard_map(
        per_device,
        mesh=mesh,
        in_specs=(
            P(("blk", "lane"), None),
            P(),
            P(None, "blk", "lane"),
            P(None, "blk", "lane"),
            P(("blk", "lane"), None, None),
            P(("blk", "lane")),
            P(("blk", "lane")),
        ),
        out_specs=P(("blk", "lane"), None),
        check_vma=False,
    )
```

```python
import functools

import jax
import jax.numpy as jnp
from jax import lax
from jax.experimental import pallas as pl
from jax.experimental.pallas import tpu as pltpu
from jax.sharding import PartitionSpec as P

MESH = pl.DeviceIdType.MESH
BLOCK = 128
TILES = 6
TAILS = 18
NZ, NX, NY = 8, 4, 2
PLANE = NX * NY
WIN = 4
ROWS, FEAT = 384, 512
NC = 4
N = FEAT // NC
SPLIT = 224
HOPS = (4, 5)
BF = jnp.bfloat16
F32 = jnp.float32


def halves(value):
    hi = value.astype(BF)
    return hi, (value - hi.astype(F32)).astype(BF)


def dot3(ah, al, bh, bl):
    def dot(a, b):
        return jnp.dot(a, b, preferred_element_type=F32)

    return dot(ah, bh) + (dot(ah, bl) + dot(al, bh))


def dot_pair(ah, al, pair):
    both = jnp.dot(ah, pair, preferred_element_type=F32)
    return (both[:, :N] + both[:, N:]) + jnp.dot(al, pair[:, :N], preferred_element_type=F32)


def kernel(
    feat_hbm, weight_hbm, hub_hbm, tail_hbm, mask, slot_tile, meta,
    out,
    fbuf, fpair, tsend, tmid, trecv, tvals, mrecv, mscal, eh, el, rpair, hubv, ah, al, hpair,
    run, crecv, hrecv, acc, zrecv, wv, wh, wl,
    load_sem, gs, gr, ts, tr, ms, mr, cs, cr, hs, hr, zs, zr, ws, wr,
):
    blk, lane = lax.axis_index("blk"), lax.axis_index("lane")
    z, p = lax.div(blk, PLANE), lax.rem(blk, PLANE)
    x, y = lax.div(p, NY), lax.rem(p, NY)
    h, c = lax.div(lane, 2), lax.rem(lane, 2)

    def at(zz, pp, hh_=None, cc=None):
        hh_ = h if hh_ is None else hh_
        cc = c if cc is None else cc
        return {"blk": lax.rem(zz + NZ, NZ) * PLANE + pp, "lane": hh_ * 2 + cc}

    def pos(xx, yy):
        return lax.rem(xx + NX, NX) * NY + yy

    def remote(src, dst, send, recv, dev):
        return pltpu.make_async_remote_copy(
            src_ref=src, dst_ref=dst, send_sem=send, recv_sem=recv, device_id=dev, device_id_type=MESH
        )

    feat_in = [
        pltpu.make_async_copy(feat_hbm.at[:, pl.ds(n * N, N)], fbuf.at[n, p], load_sem.at[n]) for n in range(NC)
    ]
    tail_in = pltpu.make_async_copy(tail_hbm, tvals.at[pl.ds(0, TAILS)], load_sem.at[NC])
    hub_in = [pltpu.make_async_copy(hub_hbm.at[s], hubv.at[s], load_sem.at[NC + 1 + s]) for s in range(3)]
    weight_in = pltpu.make_async_copy(weight_hbm, wv, load_sem.at[NC + 4])
    meta_in = pltpu.make_async_copy(meta.at[p], mrecv.at[p], load_sem.at[NC + 5])
    feat_in[0].start()
    tail_in.start()
    meta_in.start()
    for copy in feat_in[1:] + hub_in + [weight_in]:
        copy.start()

    barrier = pltpu.get_barrier_semaphore()
    partners = [at(z, lax.rem(p + i, PLANE)) for i in range(1, PLANE)]
    partners += [at(z + 1, p), at(z - 1, p), at(z + 3, p), at(z - 3, p), at(z, p, h, 1 - c), at(z, p, 1 - h, c)]
    for dev in partners:
        pl.semaphore_signal(barrier, inc=1, device_id=dev, device_id_type=MESH)
    pl.semaphore_wait(barrier, len(partners))

    yn, left, right = pos(x, 1 - y), pos(x - 1, y), pos(x + 1, y)
    right_yn = pos(x + 1, 1 - y)
    flows = [(p, yn), (p, right), (p, left), (yn, right), (yn, left), (left, right), (right_yn, left)]

    def gather(n, i):
        slot, dest = flows[i]
        return remote(fbuf.at[n, slot], fbuf.at[n, slot], gs.at[n, i], gr.at[n, i], at(z, dest))

    gathers = [[gather(n, i) for i in range(7)] for n in range(NC)]

    def first_sends(n):
        feat_in[n].wait()
        for i in range(3):
            gathers[n][i].start()

    wraps = [
        remote(fbuf.at[n, 6 + y], fbuf.at[n, 9 - y], ws.at[n, 0], wr.at[n, 0], at(z + 1, p)) for n in range(NC)
    ]
    wraps_on = [remote(fbuf.at[n, 8], fbuf.at[n, 8], ws.at[n, 1], wr.at[n, 1], at(z, yn)) for n in range(NC)]

    first_sends(0)

    tail_in.wait()
    tvals[TAILS] = jnp.zeros((BLOCK, BLOCK), F32)
    meta_copies = []
    for i in range(1, PLANE):
        q = lax.rem(p + i, PLANE)
        meta_copies.append(remote(meta.at[q], mrecv.at[p], ms.at[i - 1], mr.at[i - 1], at(z, q)))
        meta_copies[-1].start()
    steps = (1, 3, 2)
    cross, direct, onward = [], [], []

    def fill(q):
        for j in range(WIN):
            tsend[q, j] = tvals[slot_tile[q * WIN + j]]

    for i, dx in enumerate(steps + (0,)):
        q = pos(x + dx, 1 - y)
        fill(q)
        landing = tmid.at[lax.rem(x + dx, NX)] if dx else trecv.at[p]
        cross.append(remote(tsend.at[q], landing, ts.at[0, i], tr.at[0, i], at(z, yn)))
        cross[-1].start()
    for i, dx in enumerate(steps):
        q = pos(x + dx, y)
        fill(q)
        direct.append(remote(tsend.at[q], trecv.at[p], ts.at[1, i], tr.at[1, i], at(z, q)))
        direct[-1].start()
        onward.append(remote(tmid.at[lax.rem(x + dx, NX)], trecv.at[yn], ts.at[2, i], tr.at[2, i], at(z, q)))

    def pass_tile(i):
        cross[i].wait_recv()
        onward[i].start()

    for j in range(WIN):
        trecv[p, j] = tvals[slot_tile[p * WIN + j]]

    def wrap_send(n):
        @pl.when(p < 2)
        def _():
            wraps[n].start()

    def wrap_forward(n):
        @pl.when(p == 1)
        def _():
            wraps[n].wait_recv()
            wraps_on[n].start()

    def second_sends(n):
        gathers[n][0].wait_recv()
        gathers[n][3].start()
        gathers[n][4].start()
        gathers[n][1].wait_recv()
        wrap_send(n)
        gathers[n][5].start()

    def third_send(n):
        gathers[n][4].wait_recv()
        gathers[n][6].start()

    def hub_tiles(s):
        hub_in[s].wait()

        def hub_rows(i, carry):
            for jj in range(3):
                present = mask[s, i, jj].astype(F32)
                rows = pl.ds(pl.multiple_of(i * BLOCK, BLOCK), BLOCK)
                hi, lo = halves(hubv[s, rows, jj * BLOCK:(jj + 1) * BLOCK] * present)
                cols = slice(s * ROWS + jj * BLOCK, s * ROWS + (jj + 1) * BLOCK)
                ah[rows, cols] = hi
                al[rows, cols] = lo
            return carry

        lax.fori_loop(0, 12, hub_rows, 0)

    second_sends(0)
    hub_tiles(0)
    pass_tile(0)
    third_send(0)
    first_sends(1)
    hub_tiles(1)
    pass_tile(1)
    hub_tiles(2)
    pass_tile(2)
    wrap_forward(0)
    weight_in.wait()
    for i in range(4):
        hi, lo = halves(wv[i * BLOCK:(i + 1) * BLOCK])
        wh[i * BLOCK:(i + 1) * BLOCK] = hi
        wl[i * BLOCK:(i + 1) * BLOCK] = lo

    order = ([4, 3, 2, 1], [1, 2, 3, 4])
    part = (slice(0, SPLIT), slice(SPLIT, ROWS))
    size = (SPLIT, ROWS - SPLIT)

    def chain(n, way, s):
        rows = pl.ds(0, size[way])
        src = acc.at[n, order[way][0], pl.ds(part[way].start, size[way])] if s == 0 else zrecv.at[n, way, s - 1, rows]
        zz = z + 1 if way == 0 else (z - 1 if s < 4 else z - 3)
        return remote(src, zrecv.at[n, way, s, rows], zs.at[n, way, s], zr.at[n, way, s], at(zz, p))

    chains = [[[chain(n, way, s) for s in range(HOPS[way])] for way in range(2)] for n in range(NC)]

    def chain_step(n, s):
        for way in range(2):
            if s < HOPS[way]:
                chains[n][way][s - 1].wait_recv()
                if s < 4:
                    rows = slice(0, size[way])
                    zrecv[n, way, s - 1, rows] = zrecv[n, way, s - 1, rows] + acc[n, order[way][s], part[way]]
                chains[n][way][s].start()

    def tail_product(n, d):
        for pp in range(PLANE):
            j = d - (p <= pp).astype(jnp.int32)
            k = mscal[pp, 0, jnp.clip(j, 0, WIN - 1)] + 3 * pp
            rpair[pp * BLOCK:(pp + 1) * BLOCK] = fpair[k]
        acc[n, d] = dot_pair(eh[d], el[d], rpair[...])

    def convert(n):
        def one(slot, carry):
            for i in range(3):
                hi, lo = halves(fbuf[n, slot, i * BLOCK:(i + 1) * BLOCK])
                fpair[slot * 3 + i, :, :N] = hi
                fpair[slot * 3 + i, :, N:] = lo
            return carry

        lax.fori_loop(0, PLANE, one, 0)

    def hub_fill(n):
        for s in range(3):
            slot = jnp.maximum(p - s, 0)
            for i in range(3):
                hpair[s * ROWS + i * BLOCK:s * ROWS + (i + 1) * BLOCK] = fpair[slot * 3 + i]

    def hub_fill_wrap(n):
        def put(s, slot):
            hi, lo = halves(fbuf[n, slot])
            hpair[s * ROWS:(s + 1) * ROWS, :N] = hi
            hpair[s * ROWS:(s + 1) * ROWS, N:] = lo

        @pl.when(p == 0)
        def _():
            wraps_on[n].wait_recv()
            put(1, 8)
            wraps[n].wait_recv()
            put(2, 9)

        @pl.when(p == 1)
        def _():
            put(2, 8)

    core_copies = [
        remote(run.at[n, 1 - c], crecv.at[n], cs.at[n], cr.at[n], at(z, p, h, 1 - c)) for n in range(NC)
    ]
    half_rows = (pl.ds(0, ROWS // 2), pl.ds(ROWS // 2, ROWS // 2))
    half_copies = [
        [
            remote(run.at[n, c, 1 - h, half_rows[i]], hrecv.at[n, half_rows[i]], hs.at[n, i], hr.at[n, i], at(z, p, 1 - h, c))
            for i in range(2)
        ]
        for n in range(NC)
    ]

    def hub_product(n):
        def quarter(i, carry):
            rows = pl.ds(pl.multiple_of(i * ROWS, BLOCK), ROWS)
            run[n, lax.rem(i, 2), lax.div(i, 2)] = dot_pair(ah[rows], al[rows], hpair[...])
            return carry

        lax.fori_loop(0, 4, quarter, 0)
        core_copies[n].start()

    def hub_sum(n):
        core_copies[n].wait_recv()
        for i in range(2):
            run[n, c, i] = run[n, c, i] + crecv[n, i]
        for copy in half_copies[n]:
            copy.start()

    def finish(n):
        for way in range(2):
            chains[n][way][-1].wait_recv()
        for copy in half_copies[n]:
            copy.wait_recv()
        for way in range(2):
            rows = part[way]
            total = (run[n, c, h, rows] + hrecv[n, rows]) + (acc[n, 0, rows] + zrecv[n, way, HOPS[way] - 1, 0:size[way]])
            hi, lo = halves(total)
            cols = slice(n * N, (n + 1) * N)
            value = dot3(hi, lo, wh[cols], wl[cols])
            if n > 0:
                value = out[rows] + value
            out[rows] = jnp.maximum(value, 0.0) if n == NC - 1 else value

    def build_tile(pp):
        cols = pl.ds(pl.multiple_of(pp * BLOCK, BLOCK), BLOCK)
        zero = jnp.zeros((ROWS, BLOCK), BF)
        empty = jnp.where(pp < p, 4, 0)
        eh[empty, pl.ds(0, ROWS), cols] = zero
        el[empty, pl.ds(0, ROWS), cols] = zero
        for j in range(WIN):
            d = j + (p <= pp).astype(jnp.int32)
            value = trecv[pp, j]
            target = mscal[pp, 1, j]
            hi = value.astype(BF).astype(F32)
            lo = value - hi
            for t in range(3):
                keep = (target == t).astype(F32)
                eh[d, t * BLOCK:(t + 1) * BLOCK, cols] = (hi * keep).astype(BF)
                el[d, t * BLOCK:(t + 1) * BLOCK, cols] = (lo * keep).astype(BF)

    meta_in.wait()
    for copy in meta_copies:
        copy.wait_recv()
    scal = pltpu.make_async_copy(mrecv, mscal, load_sem.at[NC + 6])
    scal.start()
    scal.wait()
    def gathered(n):
        for i in (2, 3, 5, 6):
            gathers[n][i].wait_recv()

    def hub_part(n):
        hub_fill(n)
        hub_fill_wrap(n)
        hub_product(n)

    build_tile(p)
    gathered(0)
    convert(0)
    hub_part(0)
    for i, dx in enumerate(steps):
        direct[i].wait_recv()
        build_tile(pos(x - dx, y))
    second_sends(1)
    first_sends(2)
    cross[3].wait_recv()
    build_tile(yn)
    third_send(1)
    wrap_forward(1)
    hub_sum(0)
    for i, dx in enumerate(steps):
        onward[i].wait_recv()
        build_tile(pos(x - dx, 1 - y))

    for n in range(NC):
        if n > 0:
            chain_step(n - 1, 1)
            if n > 1:
                chain_step(n - 2, 4)
            if n + 1 < NC:
                second_sends(n + 1)
            gathered(n)
            convert(n)
        tail_product(n, 4)
        chains[n][0][0].start()
        tail_product(n, 1)
        chains[n][1][0].start()
        if n == NC - 1:
            break
        if n > 0:
            chain_step(n - 1, 2)
            third_send(n + 1)
            if n + 2 < NC:
                first_sends(n + 2)
        if n > 0:
            hub_part(n)
        tail_product(n, 3)
        tail_product(n, 2)
        tail_product(n, 0)
        if n > 0:
            wrap_forward(n + 1)
            hub_sum(n)
            chain_step(n - 1, 3)
        if n > 1:
            finish(n - 2)

    last = NC - 1
    tail_product(last, 3)
    tail_product(last, 2)
    chain_step(last - 1, 2)
    hub_fill(last)
    hub_fill_wrap(last)
    chain_step(last, 1)
    hub_product(last)
    chain_step(last - 1, 3)
    chain_step(last, 2)
    hub_sum(last)
    tail_product(last, 0)
    chain_step(last - 1, 4)
    chain_step(last, 3)
    finish(last - 2)
    chain_step(last, 4)
    finish(last - 1)
    finish(last)

    for n in range(NC):
        for copy in gathers[n]:
            copy.wait_send()
        for way in range(2):
            for copy in chains[n][way]:
                copy.wait_send()
        core_copies[n].wait_send()
        for copy in half_copies[n]:
            copy.wait_send()

        @pl.when(p < 2)
        def _():
            wraps[n].wait_send()

        @pl.when(p == 1)
        def _():
            wraps_on[n].wait_send()

    for copy in cross + direct + onward + meta_copies:
        copy.wait_send()


def slot_tables(tail_reader, tail_target):
    blk = lax.axis_index("blk")
    z, p = blk // PLANE, blk % PLANE
    q = jnp.arange(PLANE * WIN, dtype=jnp.int32) // WIN
    j = jnp.arange(PLANE * WIN, dtype=jnp.int32) % WIN
    reader = ((z + j + (q <= p)) % NZ) * PLANE + q
    found = (tail_reader[None, :] == reader[:, None]).astype(jnp.int32)
    tiles = jnp.arange(TAILS, dtype=jnp.int32)
    tile = jnp.sum(found * (tiles - TAILS)[None, :], 1) + TAILS
    source = jnp.sum(found * (tiles // TILES)[None, :], 1)
    target = jnp.sum(found * tail_target[None, :], 1)
    meta = jnp.stack([source.reshape(PLANE, WIN), target.reshape(PLANE, WIN)], 1)
    meta = jnp.pad(meta, ((0, 0), (0, 6), (0, BLOCK - WIN)))
    return tile, meta


def per_device(features, weight, hub_values, hub_mask, tail_values, tail_reader, tail_target):
    tile, meta = slot_tables(tail_reader, tail_target)
    dma = pltpu.SemaphoreType.DMA
    any_ = pl.BlockSpec(memory_space=pl.ANY)
    vmem = pl.BlockSpec(memory_space=pltpu.VMEM)
    smem = pl.BlockSpec(memory_space=pltpu.SMEM)
    return pl.pallas_call(
        kernel,
        out_shape=jax.ShapeDtypeStruct((ROWS, FEAT), F32),
        in_specs=[any_, any_, any_, any_, smem, smem, vmem],
        out_specs=vmem,
        scratch_shapes=[
            pltpu.VMEM((NC, 10, ROWS, N), F32),
            pltpu.VMEM((24, BLOCK, 2 * N), BF),
            pltpu.VMEM((PLANE, WIN, BLOCK, BLOCK), F32),
            pltpu.VMEM((NX, WIN, BLOCK, BLOCK), F32),
            pltpu.VMEM((PLANE, WIN, BLOCK, BLOCK), F32),
            pltpu.VMEM((TAILS + 1, BLOCK, BLOCK), F32),
            pltpu.VMEM((PLANE, 8, BLOCK), jnp.int32),
            pltpu.SMEM((PLANE, 8, BLOCK), jnp.int32),
            pltpu.VMEM((5, ROWS, PLANE * BLOCK), BF),
            pltpu.VMEM((5, ROWS, PLANE * BLOCK), BF),
            pltpu.VMEM((PLANE * BLOCK, 2 * N), BF),
            pltpu.VMEM((3, 4 * ROWS, ROWS), F32),
            pltpu.VMEM((4 * ROWS, 3 * ROWS), BF),
            pltpu.VMEM((4 * ROWS, 3 * ROWS), BF),
            pltpu.VMEM((3 * ROWS, 2 * N), BF),
            pltpu.VMEM((NC, 2, 2, ROWS, N), F32),
            pltpu.VMEM((NC, 2, ROWS, N), F32),
            pltpu.VMEM((NC, ROWS, N), F32),
            pltpu.VMEM((NC, 5, ROWS, N), F32),
            pltpu.VMEM((NC, 2, 5, max(SPLIT, ROWS - SPLIT), N), F32),
            pltpu.VMEM((FEAT, FEAT), F32),
            pltpu.VMEM((FEAT, FEAT), BF),
            pltpu.VMEM((FEAT, FEAT), BF),
            dma((NC + 7,)),
            dma((NC, 7)),
            dma((NC, 7)),
            dma((3, 4)),
            dma((3, 4)),
            dma((7,)),
            dma((7,)),
            dma((NC,)),
            dma((NC,)),
            dma((NC, 2)),
            dma((NC, 2)),
            dma((NC, 2, 5)),
            dma((NC, 2, 5)),
            dma((NC, 2)),
            dma((NC, 2)),
        ],
        compiler_params=pltpu.CompilerParams(
            collective_id=0, has_side_effects=True, vmem_limit_bytes=62 << 20
        ),
    )(features, weight, hub_values, tail_values, hub_mask, tile, meta)


def solution(mesh):
    return jax.shard_map(
        per_device,
        mesh=mesh,
        in_specs=(
            P(("blk", "lane"), None),
            P(),
            P(None, "blk", "lane"),
            P(None, "blk", "lane"),
            P(("blk", "lane"), None, None),
            P(("blk", "lane")),
            P(("blk", "lane")),
        ),
        out_specs=P(("blk", "lane"), None),
        check_vma=False,
    )
```
